256 devices in a mesh: dp: 8 (over y, core), mp: 32 (over z, x).
Axes of the slice: x: 4, y: 4, z: 8, core: 2. Of those that a mesh axis runs over, the one named last changes fastest.
Arguments:
- gradient: float32 [8192, 16384], P(('dp', 'mp')), may hold values from -2000 to 2000
- left_basis: float32 [8192, 1024], P(('dp', 'mp')), may hold values from -1 to 1, as said below
- left_values: float32 [8192], P(('dp', 'mp')), may hold values from 0.05 to 2
- right_candidates: float32 [8, 16384, 256], P('dp', 'mp'), may hold values from -1 to 1, as said below
- right_owner: int32 [64], P('mp'), may hold values from 0 to 7
- right_values: float32 [16384], P('mp'), may hold values from 0.05 to 2
Outputs:
- direction: float32 [8192, 16384], P(('dp', 'mp'))
The draws below stay inside these ranges and needn't reach their ends.
Inputs may be any that keep to these rules, and one draw needn't show every extreme that they name: Each block of 1024 rows of left_basis is an orthogonal 1024 x 1024 matrix. For every data group, each block of 256 rows of right_candidates is an orthogonal 256 x 256 matrix. right_owner[j] names the data group whose copy of column block j is current.
All inputs are finite; a program needn't handle non-finite values.
Results may differ from the reference program's by a relative error of at most 0.00011.
Values sent between devices are 32-bit elements; how exact they have to be, the bound alone decides.
No kernel may reach another device: no remote copies, remote signals or barrier semaphores. Data moves between devices by JAX's collectives and lax.ppermute only.
A program may use at most 64 MiB of HBM per device.

```python
import math
import jax
import jax.numpy as jnp
from jax import lax

D = 8192
FW = 16384
BL = 1024
BR = 256
N_DP = 8


def orthogonal_blocks(key, number, size):
    normals = jax.random.normal(key, (number, size, size), jnp.float32)
    factor, upper = jnp.linalg.qr(normals)
    return factor


def draw_gradient(key, part):
    key_values, key_rows, key_cols = jax.random.split(jax.random.fold_in(key, 7), 3)
    ramp = jnp.arange(D, dtype=jnp.float32) / (D - 1)
    row_scale = jnp.exp(jax.random.uniform(key_rows, (D,), jnp.float32, 0.0, math.log(10.0)))
    col_scale = jnp.exp(jax.random.uniform(key_cols, (FW,), jnp.float32, 0.0, math.log(10.0)))
    values = jnp.clip(jax.random.normal(key_values, (D, FW), jnp.float32), -6.0, 6.0)
    row_scale = row_scale * jnp.exp(math.log(3.0) * 0.5 * ramp)
    return values * row_scale[:, None] * col_scale[None, :]


def draw_left_basis(key, part):
    blocks = orthogonal_blocks(jax.random.fold_in(key, 11), D // BL, BL)
    return blocks.reshape(D, BL)


def draw_right_candidates(key, part):
    blocks = orthogonal_blocks(jax.random.fold_in(key, 13), N_DP * (FW // BR), BR)
    return blocks.reshape(N_DP, FW, BR)


def place_ends(values, rng, least, top_value):
    extent = values.shape
    place = [jax.random.randint(jax.random.fold_in(rng, axis), (), 0, extent[axis]) for axis in range(len(extent))]
    values = values.at[tuple(place)].set(least)
    longest = extent.index(max(extent))
    place[longest] = (place[longest] + 1) % extent[longest]
    return values.at[tuple(place)].set(top_value)


def shard_levels(rng, dims, shards, least, high):
    gain, own = 1.0, jax.random.fold_in(rng, 6)
    for dim, parts in shards:
        steps = jnp.exp(jax.random.uniform(jax.random.fold_in(own, dim), (parts,), jnp.float32, least / len(shards), high / len(shards)))
        gain = gain * jnp.repeat(steps, dims[dim] // parts).reshape([-1 if axis == dim else 1 for axis in range(len(dims))])
    return gain


def setup_inputs(seed: int = 0) -> dict:
    keys = jax.random.split(jax.random.key(seed), 7)
    return {
        "gradient": draw_gradient(jax.random.fold_in(keys[6], 71), 0),
        "left_basis": draw_left_basis(jax.random.fold_in(keys[6], 71), 0),
        "left_values": jnp.clip(jnp.exp(math.log(2.0) - 3.6888794 * jax.random.uniform(keys[2], (D,), jnp.float32) ** shard_levels(keys[2], (D,), ((0, 256),), -0.2, 0.2)), 0.05, 2.0),
        "right_candidates": draw_right_candidates(jax.random.fold_in(keys[6], 71), 0),
        "right_owner": place_ends(jax.random.randint(keys[4], (FW // BR,), 0, N_DP), jax.random.fold_in(keys[4], 1), 0, N_DP - 1).astype(jnp.int32),
        "right_values": jnp.clip(jnp.exp(math.log(2.0) - 3.6888794 * jax.random.uniform(keys[5], (FW,), jnp.float32) ** shard_levels(keys[5], (FW,), ((0, 32),), -0.2, 0.2)), 0.05, 2.0),
    }


damping = 0.01
epsilon = 1e-06
highest = lax.Precision.HIGHEST

def reference(gradient, left_basis, left_values, right_candidates, right_owner, right_values):
    left_count = D // BL
    right_count = FW // BR
    left_cubes = left_basis.reshape(left_count, BL, BL)
    stacked = right_candidates.reshape(N_DP, right_count, BR, BR)
    right_bases = stacked[right_owner, jnp.arange(right_count, dtype=jnp.int32)]
    right_lam = right_values.reshape(right_count, BR)
    grad_slabs = gradient.reshape(left_count, BL, right_count, BR)
    lam_slabs = left_values.reshape(left_count, BL)

    def one_block(inputs):
        left_block, grad_slab, lam_rows = inputs
        rotated = jnp.einsum('ra,rjc->ajc', left_block, grad_slab, precision=highest)
        rotated = jnp.einsum('ajc,jcd->ajd', rotated, right_bases, precision=highest)
        scaled = rotated / (lam_rows[:, None, None] + right_lam[None] + damping)
        restored = jnp.einsum('ajd,jcd->ajc', scaled, right_bases, precision=highest)
        return jnp.einsum('ra,ajc->rjc', left_block, restored, precision=highest)
    result = lax.map(one_block, (left_cubes, grad_slabs, lam_slabs)).reshape(D, FW)
    mean_square = jnp.sum(result * result) / (D * FW)
    return result * lax.rsqrt(mean_square + epsilon)
```

```python
import jax
import jax.numpy as jnp
from jax import lax
from jax.experimental import pallas as pl
from jax.experimental.pallas import tpu as pltpu
from jax.sharding import Mesh
from jax.sharding import PartitionSpec as P

D = 8192
FW = 16384
BL = 1024
BR = 256
NY, NC, NZ, NX = 4, 2, 8, 4
N_MP = NZ * NX
ROWS = D // (NY * NC * N_MP)
SPAN = FW // N_MP
CHUNKS = SPAN // BR
MP = ("z", "x")
DP = ("y", "c")
DP_MP = ("y", "c", "z", "x")
TILES = ROWS * BL // 1024
PIECE = (TILES + 1) * 8

damping = 0.01
epsilon = 1e-06
f32 = jnp.float32
bf16 = jnp.bfloat16


def ring(n, step):
    return [(i, (i + step) % n) for i in range(n)]


def struct(shape, dtype=f32):
    return jax.ShapeDtypeStruct(shape, dtype)


def vmem():
    return pl.BlockSpec(memory_space=pltpu.VMEM)


def params(mebibytes):
    return pltpu.CompilerParams(vmem_limit_bytes=mebibytes * 1024 * 1024)


def cost(flops, moved):
    return pl.CostEstimate(flops=flops, bytes_accessed=moved, transcendentals=0)


def spread_columns(gradient):
    def kernel(g_ref, *refs):
        sems = refs[NX]
        x = lax.axis_index("x")
        copies = []
        for distance in range(NX):
            for z in range(NZ):
                dest = z * NX + lax.rem(x + distance, NX)
                copy = pltpu.make_async_copy(
                    g_ref.at[:, pl.ds(pl.multiple_of(dest * SPAN, SPAN), SPAN)],
                    refs[distance].at[z],
                    sems.at[distance * NZ + z],
                )
                copy.start()
                copies.append(copy)
        for copy in copies:
            copy.wait()

    return pl.pallas_call(
        kernel,
        out_shape=[struct((NZ, ROWS, SPAN))] * NX,
        in_specs=[pl.BlockSpec(memory_space=pltpu.HBM)],
        out_specs=[vmem()] * NX,
        scratch_shapes=[pltpu.SemaphoreType.DMA((N_MP,))],
        compiler_params=params(8),
        cost_estimate=cost(0, 2 * ROWS * FW * 4),
        name="spread_columns",
    )(gradient)


def merge_columns(blocks):
    def kernel(*refs):
        for distance in range(NX):
            refs[NX][:, distance] = refs[distance][...]

    return pl.pallas_call(
        kernel,
        out_shape=struct((NZ, NX, ROWS, SPAN)),
        in_specs=[vmem()] * NX,
        out_specs=vmem(),
        compiler_params=params(8),
        cost_estimate=cost(0, 2 * ROWS * FW * 4),
        name="merge_columns",
    )(*blocks)


def stack_column(pairs):
    def kernel(*refs):
        out = refs[len(pairs)]
        z = lax.axis_index("z")
        for pair, distance in zip(refs, (0, 1, 2, NZ - 1)):
            for member in range(2):
                at = lax.rem(z + NZ - distance + member * (NZ // 2), NZ)
                out[pl.ds(at, 1)] = pair[member : member + 1]

    return pl.pallas_call(
        kernel,
        out_shape=struct((NZ, PIECE, 128)),
        in_specs=[vmem()] * len(pairs),
        out_specs=vmem(),
        compiler_params=params(8),
        cost_estimate=cost(0, 2 * NZ * PIECE * 128 * 4),
        name="stack_column",
    )(*pairs)


def split_piece(*parts):
    count = len(parts)

    def kernel(*refs):
        high_ref, low_ref, values_ref = refs[count:]
        row = 0
        for part in refs[:count]:
            for z in range(part.shape[0]):
                lines = []
                for r in range(ROWS // 8):
                    tiles = [
                        part[z, (r * (BL // 128) + t) * 8 : (r * (BL // 128) + t + 1) * 8, :]
                        for t in range(BL // 128)
                    ]
                    lines.append(jnp.concatenate(tiles, axis=1))
                whole = jnp.concatenate(lines, axis=0)
                high = whole.astype(bf16)
                low = (whole - high.astype(f32)).astype(bf16)
                high_ref[row * ROWS : (row + 1) * ROWS, :] = high
                low_ref[row * ROWS : (row + 1) * ROWS, :] = low
                values_ref[row : row + 1, :] = part[z, TILES * 8 : TILES * 8 + 1, :]
                row += 1

    return pl.pallas_call(
        kernel,
        out_shape=[struct((NZ * ROWS, BL), bf16), struct((NZ * ROWS, BL), bf16), struct((NZ, 128))],
        in_specs=[vmem()] * count,
        out_specs=[vmem()] * 3,
        compiler_params=params(8),
        cost_estimate=cost(0, 2 * NZ * PIECE * 128 * 4),
        name="split_piece",
    )(*parts)


def halves(x):
    high = x.astype(bf16)
    return high, (x - high.astype(f32)).astype(bf16)


def product(a, b, dims):
    dot = lambda u, v: lax.dot_general(u, v, (dims, ((), ())), preferred_element_type=f32)
    return dot(a[0], b[0]) + (dot(a[0], b[1]) + dot(a[1], b[0]))


def rotate_and_scale(columns, pieces, rights, right_values):
    def kernel(g_ref, *refs):
        left = [refs[3 * p : 3 * p + 3] for p in range(NX)]
        right_refs, values_ref, high_ref, low_ref, total_ref = (
            refs[3 * NX : 3 * NX + CHUNKS],
            *refs[3 * NX + CHUNKS :],
        )
        tiles = left[0][2][...] + left[1][2][...] + left[2][2][...] + left[3][2][...]
        row_values = jnp.concatenate([tiles[z : z + 1, :] for z in range(NZ)], axis=1)
        total = jnp.zeros((8, 128), f32)
        for chunk in range(CHUNKS):
            at = slice(chunk * BR, (chunk + 1) * BR)
            rotated = None
            for p in range(NX):
                g = g_ref[:, p, :, at].reshape(NZ * ROWS, BR)
                term = product(halves(g.T), (left[p][0][...], left[p][1][...]), ((1,), (0,)))
                rotated = term if rotated is None else rotated + term
            right = right_refs[chunk][...]
            turned = product(halves(right.T), halves(rotated), ((1,), (0,)))
            scaled = turned / (row_values + values_ref[at, :] + damping)
            square = scaled * scaled
            for r in range(BR // 8):
                for t in range(BL // 128):
                    total = total + square[r * 8 : (r + 1) * 8, t * 128 : (t + 1) * 128]
            restored = product(halves(right), halves(scaled), ((1,), (0,)))
            high_ref[:, at], low_ref[:, at] = halves(restored.T)
        total_ref[...] = total

    flat = [array for piece in pieces for array in piece]
    return pl.pallas_call(
        kernel,
        out_shape=[struct((BL, SPAN), bf16)] * 2 + [struct((8, 128))],
        in_specs=[vmem()] * (2 + CHUNKS + len(flat)),
        out_specs=[vmem()] * 3,
        compiler_params=params(16),
        cost_estimate=cost(6 * BL * SPAN * (BL + 2 * BR), 8 * BL * BL),
        name="rotate_and_scale",
    )(columns, *flat, *rights, right_values)


def rotate_back(high, low, pieces):
    def kernel(high_ref, low_ref, *refs):
        out_ref = refs[2 * NX]
        x = lax.axis_index("x")
        back = high_ref[...], low_ref[...]
        for p in range(NX):
            left = refs[2 * p][...], refs[2 * p + 1][...]
            rows = product(left, back, ((1,), (0,)))
            out_ref[:, pl.ds(lax.rem(x + NX - p, NX), 1)] = rows.reshape(NZ, 1, ROWS, SPAN)

    flat = [array for piece in pieces for array in piece[:2]]
    return pl.pallas_call(
        kernel,
        out_shape=struct((NZ, NX, ROWS, SPAN)),
        in_specs=[vmem()] * (2 + len(flat)),
        out_specs=vmem(),
        compiler_params=params(16),
        cost_estimate=cost(6 * BL * SPAN * BL, 8 * BL * BL),
        name="rotate_back",
    )(high, low, *flat)


def join_rows(result, total):
    def kernel(total_ref, in_ref, out_ref, scaled, sems):
        whole = jnp.sum(jnp.sum(total_ref[...], axis=0, keepdims=True), axis=1, keepdims=True)
        scale = lax.rsqrt(whole / (D * FW) + epsilon)
        copies = []
        for block in range(N_MP):
            scaled[block] = in_ref[block] * scale
            copy = pltpu.make_async_copy(
                scaled.at[block], out_ref.at[:, block * SPAN : (block + 1) * SPAN], sems.at[block]
            )
            copy.start()
            copies.append(copy)
        for copy in copies:
            copy.wait()

    return pl.pallas_call(
        kernel,
        out_shape=struct((ROWS, FW)),
        in_specs=[vmem()] * 2,
        out_specs=pl.BlockSpec(memory_space=pl.ANY),
        scratch_shapes=[pltpu.VMEM((N_MP, ROWS, SPAN), f32), pltpu.SemaphoreType.DMA((N_MP,))],
        compiler_params=params(8),
        cost_estimate=cost(ROWS * FW, 2 * ROWS * FW * 4),
        name="join_rows",
    )(total, result)


def gather_column(left_basis, left_values):
    by_tile = left_basis.reshape(ROWS // 8, 8, BL // 128, 128).transpose(0, 2, 1, 3)
    values = lax.dynamic_update_slice(
        jnp.zeros((8, 128), f32), left_values[None], (0, lax.axis_index("x") * ROWS)
    )
    shard = jnp.concatenate([by_tile.reshape(TILES * 8, 128), values])
    pair = jnp.stack([shard, lax.ppermute(shard, "z", ring(NZ, NZ // 2))])
    return [pair] + [lax.ppermute(pair, "z", ring(NZ, step)) for step in (1, 2, -1)]


def current_right(candidates, owner):
    c, y = lax.axis_index("c"), lax.axis_index("y")
    source = jnp.where(c == 0, owner[0], owner[1])
    mine = jnp.where(c == 0, candidates[0], candidates[1])
    other = jnp.where(c == 0, candidates[1], candidates[0])
    received = lax.ppermute(other, "c", ring(NC, 1))
    chosen = block = jnp.where(source % NC == c, mine, received)
    distance = lax.rem(y + NY - source // NC, NY)
    for k in range(1, NY):
        chosen = jnp.where(distance == k, lax.ppermute(block, "y", ring(NY, k)), chosen)
    partner = lax.ppermute(chosen, "c", ring(NC, 1))
    return jnp.where(c == 0, chosen, partner), jnp.where(c == 0, partner, chosen)


def total_over_devices(value):
    for axis, n, distances in (("c", NC, 2), ("y", NY, NY), ("x", NX, NX), ("z", NZ, NZ // 2)):
        terms = [lax.ppermute(value, axis, ring(n, k)) for k in range(1, distances)]
        for term in terms:
            value = value + term
    return value


def on_device(gradient, left_basis, left_values, right_candidates, right_owner, right_values):
    blocks = spread_columns(gradient)
    blocks = [blocks[0]] + [lax.ppermute(blocks[k], "x", ring(NX, k)) for k in range(1, NX)]
    send = merge_columns(blocks)
    pairs = gather_column(left_basis, left_values)
    column = stack_column(pairs)
    own = split_piece(column)
    send, *own = lax.optimization_barrier((send, *own))
    columns = lax.all_to_all(send, "z", split_axis=0, concat_axis=0, tiled=True)
    before = lax.ppermute(column, "x", ring(NX, 1))
    after = lax.ppermute(column, "x", ring(NX, -1))
    rights = current_right(right_candidates.reshape(CHUNKS, BR, BR), right_owner)
    half = NZ // 2
    far_low = lax.ppermute(before[:half], "x", ring(NX, 1))
    far_high = lax.ppermute(after[half:], "x", ring(NX, -1))
    pieces = [
        own,
        split_piece(before),
        split_piece(far_low, far_high),
        split_piece(after),
    ]
    high, low, squares = rotate_and_scale(
        columns, pieces, rights, right_values.reshape(SPAN, 1)
    )
    squares = squares + lax.ppermute(squares, "z", ring(NZ, NZ // 2))
    result = rotate_back(high, low, pieces)
    result, squares = lax.optimization_barrier((result, squares))
    back = lax.all_to_all(
        result.reshape(N_MP, ROWS, SPAN), MP, split_axis=0, concat_axis=0, tiled=True
    )
    return join_rows(back, total_over_devices(squares))


def solution(mesh):
    split = Mesh(mesh.devices.reshape(NY, NC, NZ, NX), DP_MP)
    return jax.shard_map(
        on_device,
        mesh=split,
        in_specs=(P(DP_MP, None), P(DP_MP, None), P(DP_MP), P(DP, MP, None), P(MP), P(MP)),
        out_specs=P(DP_MP, None),
        check_vma=False,
    )
```

```python
import jax
import jax.numpy as jnp
from jax import lax
from jax.experimental import pallas as pl
from jax.experimental.pallas import tpu as pltpu
from jax.sharding import Mesh
from jax.sharding import PartitionSpec as P

D = 8192
FW = 16384
BL = 1024
BR = 256
NY, NC, NZ, NX = 4, 2, 8, 4
N_MP = NZ * NX
ROWS = D // (NY * NC * N_MP)
SPAN = FW // N_MP
CHUNKS = SPAN // BR
MP = ("z", "x")
DP = ("y", "c")
DP_MP = ("y", "c", "z", "x")
TILES = ROWS * BL // 1024
PIECE = (TILES + 1) * 8

damping = 0.01
epsilon = 1e-06
f32 = jnp.float32
bf16 = jnp.bfloat16


def ring(n, step):
    return [(i, (i + step) % n) for i in range(n)]


def struct(shape, dtype=f32):
    return jax.ShapeDtypeStruct(shape, dtype)


def vmem():
    return pl.BlockSpec(memory_space=pltpu.VMEM)


def params(mebibytes):
    return pltpu.CompilerParams(vmem_limit_bytes=mebibytes * 1024 * 1024)


def cost(flops, moved):
    return pl.CostEstimate(flops=flops, bytes_accessed=moved, transcendentals=0)


def hbm():
    return pl.BlockSpec(memory_space=pl.ANY)


def spread(gradient):
    def kernel(g_ref, out_ref, rows_ref, in_sems, out_sems):
        fetches, stores = [], []
        for z in range(NZ):
            at = slice(z * NX * SPAN, (z + 1) * NX * SPAN)
            copy = pltpu.make_async_copy(g_ref.at[:, at], rows_ref.at[:, at], in_sems.at[z])
            copy.start()
            fetches.append(copy)
        for z in range(NZ):
            fetches[z].wait()
            for x in range(NX):
                dest = z * NX + x
                copy = pltpu.make_async_copy(
                    rows_ref.at[:, dest * SPAN : (dest + 1) * SPAN],
                    out_ref.at[x, z],
                    out_sems.at[dest],
                )
                copy.start()
                stores.append(copy)
        for copy in stores:
            copy.wait()

    return pl.pallas_call(
        kernel,
        out_shape=struct((NX, NZ, ROWS, SPAN)),
        in_specs=[hbm()],
        out_specs=hbm(),
        scratch_shapes=[
            pltpu.VMEM((ROWS, FW), f32),
            pltpu.SemaphoreType.DMA((NZ,)),
            pltpu.SemaphoreType.DMA((N_MP,)),
        ],
        compiler_params=params(56),
        cost_estimate=cost(0, 2 * ROWS * FW * 4),
        name="spread",
    )(gradient)


def make_shard(left_basis, values):
    def kernel(left_ref, values_ref, shard_ref):
        for r in range(ROWS // 8):
            for t in range(BL // 128):
                at = (r * (BL // 128) + t) * 8
                shard_ref[at : at + 8, :] = left_ref[r * 8 : r * 8 + 8, t * 128 : t * 128 + 128]
        shard_ref[TILES * 8 :, :] = values_ref[...]

    return pl.pallas_call(
        kernel,
        out_shape=struct((PIECE, 128)),
        in_specs=[vmem(), vmem()],
        out_specs=vmem(),
        compiler_params=params(8),
        cost_estimate=cost(0, 2 * ROWS * BL * 4),
        name="make_shard",
    )(left_basis, values)


def merge_columns(blocks):
    def kernel(in_ref, out_ref):
        for x in range(NX):
            out_ref[:, x] = in_ref[x]

    return pl.pallas_call(
        kernel,
        out_shape=struct((NZ, NX, ROWS, SPAN)),
        in_specs=[vmem()],
        out_specs=vmem(),
        compiler_params=params(8),
        cost_estimate=cost(0, 2 * ROWS * FW * 4),
        name="merge_columns",
    )(blocks)


def stack_column(shards):
    half = NZ // 2

    def kernel(*refs):
        low, high = refs[len(shards) :]
        z = lax.axis_index("z")
        for ref, distances in zip(refs, DISTANCES):
            for member, distance in enumerate(distances):
                at = lax.rem(z + NZ - distance, NZ)
                value = ref[member : member + 1] if len(distances) > 1 else ref[...][None]

                @pl.when(at < half)
                def _():
                    low[pl.ds(at, 1)] = value

                @pl.when(at >= half)
                def _():
                    high[pl.ds(at - half, 1)] = value

    return pl.pallas_call(
        kernel,
        out_shape=[struct((half, PIECE, 128))] * 2,
        in_specs=[vmem()] * len(shards),
        out_specs=[vmem()] * 2,
        compiler_params=params(8),
        cost_estimate=cost(0, 2 * NZ * PIECE * 128 * 4),
        name="stack_column",
    )(*shards)


def halves(x):
    high = x.astype(bf16)
    return high, (x - high.astype(f32)).astype(bf16)


def product(a, b, dims):
    dot = lambda u, v: lax.dot_general(u, v, (dims, ((), ())), preferred_element_type=f32)
    return dot(a[0], b[0]) + (dot(a[0], b[1]) + dot(a[1], b[0]))


def precondition(columns, pieces, rights, right_values):
    half = NZ // 2
    count = 2 * NX

    def kernel(columns_ref, *refs):
        piece_refs, right_refs = refs[:count], refs[count : count + CHUNKS]
        (values_ref, out_ref, total_ref, columns, tiles, left, rows_ref, in_sems, out_sems) = refs[
            count + CHUNKS :
        ]
        x = lax.axis_index("x")
        owns = [lax.rem(x + NX - p, NX) for p in range(NX)]
        fetches = []
        for p in range(NX):
            for h in range(2):
                number = 2 * p + h
                fetches.append(
                    pltpu.make_async_copy(piece_refs[number], tiles.at[number], in_sems.at[number])
                )
            fetches.append(
                pltpu.make_async_copy(
                    columns_ref.at[:, owns[p]], columns.at[p], in_sems.at[count + p]
                )
            )
        for copy in fetches:
            copy.start()
        rotated = None
        row_values = [jnp.zeros((1, 128), f32)] * NZ
        for p in range(NX):
            for copy in fetches[3 * p : 3 * p + 3]:
                copy.wait()
            for z in range(NZ):
                part = 2 * p + z // half
                lines = []
                for r in range(ROWS // 8):
                    first = r * (BL // 128) * 8
                    lines.append(
                        jnp.concatenate(
                            [
                                tiles[part, z % half, first + t * 8 : first + t * 8 + 8, :]
                                for t in range(BL // 128)
                            ],
                            axis=1,
                        )
                    )
                at = slice(z * ROWS, (z + 1) * ROWS)
                left[p, 0, at, :], left[p, 1, at, :] = halves(jnp.concatenate(lines, axis=0))
                row_values[z] = row_values[z] + tiles[part, z % half, TILES * 8 : TILES * 8 + 1, :]
            g = columns[p].reshape(NZ * ROWS, SPAN)
            term = product(halves(g.T), (left[p, 0], left[p, 1]), ((1,), (0,)))
            rotated = term if rotated is None else rotated + term
        row_values = jnp.concatenate(row_values, axis=1)
        total = jnp.zeros((8, 128), f32)
        backs = []
        for chunk in range(CHUNKS):
            at = slice(chunk * BR, (chunk + 1) * BR)
            right = right_refs[chunk][...]
            turned = product(halves(right.T), halves(rotated[at, :]), ((1,), (0,)))
            scaled = turned / (row_values + values_ref[at, :] + damping)
            square = scaled * scaled
            for r in range(BR // 8):
                for t in range(BL // 128):
                    total = total + square[r * 8 : (r + 1) * 8, t * 128 : (t + 1) * 128]
            restored = product(halves(right), halves(scaled), ((1,), (0,)))
            backs.append(halves(restored.T))
        total_ref[...] = total
        back = [jnp.concatenate([b[part] for b in backs], axis=1) for part in range(2)]
        stores = []
        for p in range(NX):
            rows = product((left[p, 0], left[p, 1]), back, ((1,), (0,)))
            rows_ref[p] = rows.reshape(NZ, ROWS, SPAN)
            copy = pltpu.make_async_copy(rows_ref.at[p], out_ref.at[:, owns[p]], out_sems.at[p])
            copy.start()
            stores.append(copy)
        for copy in stores:
            copy.wait()

    return pl.pallas_call(
        kernel,
        out_shape=[struct((NZ, NX, ROWS, SPAN)), struct((8, 128))],
        in_specs=[hbm()] * (1 + count) + [vmem()] * (CHUNKS + 1),
        out_specs=[hbm(), vmem()],
        scratch_shapes=[
            pltpu.VMEM((NX, NZ, ROWS, SPAN), f32),
            pltpu.VMEM((count, half, PIECE, 128), f32),
            pltpu.VMEM((NX, 2, NZ * ROWS, BL), bf16),
            pltpu.VMEM((NX, NZ, ROWS, SPAN), f32),
            pltpu.SemaphoreType.DMA((count + NX,)),
            pltpu.SemaphoreType.DMA((NX,)),
        ],
        compiler_params=params(56),
        cost_estimate=cost(12 * BL * SPAN * (BL + BR), 8 * BL * BL),
        name="precondition",
    )(columns, *pieces, *rights, right_values)


def join_rows(result, total):
    def kernel(total_ref, in_ref, out_ref, scaled, sems):
        whole = jnp.sum(jnp.sum(total_ref[...], axis=0, keepdims=True), axis=1, keepdims=True)
        scale = lax.rsqrt(whole / (D * FW) + epsilon)
        copies = []
        for block in range(N_MP):
            scaled[block] = in_ref[block] * scale
            copy = pltpu.make_async_copy(
                scaled.at[block], out_ref.at[:, block * SPAN : (block + 1) * SPAN], sems.at[block]
            )
            copy.start()
            copies.append(copy)
        for copy in copies:
            copy.wait()

    return pl.pallas_call(
        kernel,
        out_shape=struct((ROWS, FW)),
        in_specs=[vmem()] * 2,
        out_specs=pl.BlockSpec(memory_space=pl.ANY),
        scratch_shapes=[pltpu.VMEM((N_MP, ROWS, SPAN), f32), pltpu.SemaphoreType.DMA((N_MP,))],
        compiler_params=params(8),
        cost_estimate=cost(ROWS * FW, 2 * ROWS * FW * 4),
        name="join_rows",
    )(total, result)


DISTANCES = ((0, NZ // 2), (2,), (NZ - 2,), (1, NZ // 2 + 1), (NZ - 1, NZ // 2 - 1))


def gather_column(shard):
    far = lax.ppermute(shard, "z", ring(NZ, NZ // 2))
    two = [lax.ppermute(shard, "z", ring(NZ, step)) for step in (2, -2)]
    pair = jnp.stack([shard, far])
    return [pair] + two + [lax.ppermute(pair, "z", ring(NZ, step)) for step in (1, -1)]


def current_right(candidates, owner):
    c, y = lax.axis_index("c"), lax.axis_index("y")
    source = jnp.where(c == 0, owner[0], owner[1])
    mine = jnp.where(c == 0, candidates[0], candidates[1])
    other = jnp.where(c == 0, candidates[1], candidates[0])
    received = lax.ppermute(other, "c", ring(NC, 1))
    chosen = block = jnp.where(source % NC == c, mine, received)
    distance = lax.rem(y + NY - source // NC, NY)
    for k in range(1, NY):
        chosen = jnp.where(distance == k, lax.ppermute(block, "y", ring(NY, k)), chosen)
    partner = lax.ppermute(chosen, "c", ring(NC, 1))
    return jnp.where(c == 0, chosen, partner), jnp.where(c == 0, partner, chosen)


def total_over_devices(value):
    value = value + lax.ppermute(value, "c", ring(NC, 1))
    for axis, n in (("y", NY), ("x", NX)):
        terms = [lax.ppermute(value, axis, ring(n, k)) for k in range(1, n)]
        for term in terms:
            value = value + term
    terms = []
    for k in range(1, NZ // 2):
        pairs = [(z, (z + k) % NZ) for z in range(NZ)] + [(NZ + z, NZ + (z - k) % NZ) for z in range(NZ)]
        terms.append(lax.ppermute(value, ("c", "z"), pairs))
    first = lax.axis_index("c") == 0
    far = lax.ppermute(value, "z", ring(NZ, NZ // 2))
    mine = jnp.where(first, value + far, 0.0)
    for term in terms:
        mine = mine + term
    return mine + lax.ppermute(mine, "c", ring(NC, 1))


def over_z(blocks):
    return lax.all_to_all(blocks, "z", split_axis=0, concat_axis=0, tiled=True)


def on_device(gradient, left_basis, left_values, right_candidates, right_owner, right_values):
    blocks = lax.all_to_all(spread(gradient), "x", split_axis=0, concat_axis=0, tiled=True)
    values = lax.dynamic_update_slice(
        jnp.zeros((8, 128), f32), left_values[None], (0, lax.axis_index("x") * ROWS)
    )
    shard = make_shard(left_basis, values)
    pairs = gather_column(shard)
    low, high = stack_column(pairs)
    send = merge_columns(blocks)
    send, low, high = lax.optimization_barrier((send, low, high))
    columns = over_z(send)
    before_low = lax.ppermute(low, "x", ring(NX, 1))
    after_high = lax.ppermute(high, "x", ring(NX, -1))
    before_high = lax.ppermute(high, "x", ring(NX, 1))
    after_low = lax.ppermute(low, "x", ring(NX, -1))
    far_low = lax.ppermute(before_low, "x", ring(NX, 1))
    far_high = lax.ppermute(after_high, "x", ring(NX, -1))
    rights = current_right(right_candidates.reshape(CHUNKS, BR, BR), right_owner)
    pieces = [low, high, before_low, before_high, far_low, far_high, after_low, after_high]
    result, squares = precondition(columns, pieces, rights, right_values.reshape(SPAN, 1))
    result = result.reshape(N_MP, ROWS, SPAN)
    back = lax.all_to_all(result, MP, split_axis=0, concat_axis=0, tiled=True)
    return join_rows(back, total_over_devices(squares))


def solution(mesh):
    split = Mesh(mesh.devices.reshape(NY, NC, NZ, NX), DP_MP)
    return jax.shard_map(
        on_device,
        mesh=split,
        in_specs=(P(DP_MP, None), P(DP_MP, None), P(DP_MP), P(DP, MP, None), P(MP), P(MP)),
        out_specs=P(DP_MP, None),
        check_vma=False,
    )
```
